256 devices in a mesh: req: 64 (over y, z_hi, x, core), dec: 4 (over z_lo).
Axes of the slice: x: 4, y: 4, z: 8 (z_hi: 2, z_lo: 4; z = z_hi * 4 + z_lo), core: 2. Of those that a mesh axis runs over, the one named last changes fastest.
Arguments:
- queries: bfloat16 [32768, 2048], P('req', 'dec')
- keys: bfloat16 [32768, 2048], P('req', 'dec'), may hold values from -6 to 6
- values: bfloat16 [32768, 2048], P('req', 'dec'), may hold values from -6 to 6
- resid: bfloat16 [32768, 2048], P('req', 'dec'), may hold values from -6 to 6
- seg_ids: int32 [32768], P('req'), may hold values from -1 to 7, as said below
- out_weight: bfloat16 [2048, 2048], P('dec'), may hold values from -0.125 to 0.125
- norm_gain: float32 [2048], replicated, may hold values from 0.1 to 1.9
- adapter_down: bfloat16 [2048, 128], replicated, may hold values from -0.125 to 0.125
- adapter_up: bfloat16 [128, 4096], P(None, ('req', 'dec')), may hold values from -0.5 to 0.5
- gate_weight: bfloat16 [2048, 4096], P(None, ('req', 'dec')), may hold values from -0.125 to 0.125
- up_weight: bfloat16 [2048, 4096], P(None, ('req', 'dec')), may hold values from -0.125 to 0.125
- down_weight: bfloat16 [4096, 2048], P(('req', 'dec')), may hold values from -0.09375 to 0.09375
- row_order: int32 [64, 512], P('req'), may hold values from 0 to 511, each once within a row
- block_table: int32 [64, 8], P('req'), may hold values from 0 to 7, each once within a row
Outputs:
- block_out: bfloat16 [32768, 2048], P('req', 'dec')
- kv_cache: bfloat16 [512, 64, 4096], P(('req', 'dec'))
The draws below stay inside these ranges and needn't reach their ends.
Inputs may be any that keep to these rules, and one draw needn't show every extreme that they name: `seg_ids`: within each index of req the live slots come first, grouped into requests whose numbers start at 0, rise by one from request to request and never fall, then come padding slots marked -1; some index of req holds one request that fills all its 512 slots, and when there is more than one index of req, some other index holds request numbers up to the stated most.
All inputs are finite; a program needn't handle non-finite values.
Results may differ from the reference program's by a relative error of at most 0.017.
Values may be sent and summed in bfloat16 or wider, within the bound.
A program may use at most 128 MiB of HBM per device.

```python
import jax
import jax.numpy as jnp
import numpy as np
from jax import lax

D = 2048
HEADS = 16
HD = 128
FF = 4096
RANK = 128
BLK = 64
CAP = 512
NB = 8
SLOTS = 32768
N_REQ = 64
N_DEC = 4


def draw_queries(key, part):
    base_key = jax.random.fold_in(key, 0)
    sample = jnp.clip(jax.random.normal(base_key, (N_REQ * CAP, HEADS * HD), jnp.float32), -6.0, 6.0)
    return sample.astype(jnp.bfloat16)


def draw_seg_ids(key, part):
    live_key, full_key, flag_key = jax.random.split(key, 3)
    devices = jnp.arange(N_REQ)
    live_count = jax.random.randint(live_key, (N_REQ,), CAP // 8, CAP + 1)
    full_device = jax.random.randint(full_key, (), 0, N_REQ)
    busy_device = (full_device + 1) % N_REQ
    live_count = jnp.where(devices == full_device, CAP, live_count)
    live_count = jnp.where(devices == busy_device, CAP, live_count)
    position = jnp.arange(CAP)
    starts = jax.random.randint(flag_key, (N_REQ, CAP), 0, 48) == 0
    starts = starts | (position[None, :] == 0)
    starts = starts | (devices[:, None] == busy_device) & (position[None, :] % 64 == 0)
    starts = starts & ((devices[:, None] != full_device) | (position[None, :] == 0))
    segment = jnp.cumsum(starts.astype(jnp.int32), axis=1) - 1
    segment = jnp.minimum(segment, CAP // 64 - 1)
    segment = jnp.where(position[None, :] < live_count[:, None], segment, -1)
    return segment.reshape(N_REQ * CAP).astype(jnp.int32)


def block_scale(own_key, extent, cuts, least, high):
    factor_of = 1.0
    for dim, blocks in cuts:
        heights = jax.random.uniform(jax.random.fold_in(jax.random.fold_in(own_key, 6), dim), (blocks,), jnp.float32, least / len(cuts), high / len(cuts))
        factor_of = factor_of * jnp.repeat(jnp.exp(heights), extent[dim] // blocks).reshape((-1,) + (1,) * (len(extent) - 1 - dim))
    return factor_of


def bell_draw(rng, dims, width, reach, pieces=(), kind=jnp.bfloat16):
    values = jax.random.normal(rng, dims, jnp.float32) * width
    if len(pieces) > 0:
        values = block_scale(rng, dims, pieces, -0.22, 0.18) * values
    return jnp.clip(values, min=-reach, max=reach).astype(kind)


def setup_inputs(seed: int = 0) -> dict:
    key_of = jax.random.split(jax.random.key(seed), 15)
    return {
        "queries": draw_queries(jax.random.fold_in(key_of[14], 71), 0),
        "keys": bell_draw(key_of[1], (SLOTS, HEADS * HD), 1.0, 6.0, ((0, 64), (1, 4))),
        "values": bell_draw(key_of[2], (SLOTS, HEADS * HD), 1.0, 6.0, ((0, 64), (1, 4))),
        "resid": bell_draw(key_of[3], (SLOTS, D), 1.0, 6.0, ((0, 64), (1, 4))),
        "seg_ids": draw_seg_ids(jax.random.fold_in(key_of[14], 71), 0),
        "out_weight": bell_draw(key_of[5], (HEADS * HD, D), (HEADS * HD) ** -0.5, 0.125, ((0, 4),)),
        "norm_gain": jnp.clip(1.0 + 0.18 * jax.random.normal(key_of[6], (D,), jnp.float32), 0.1, 1.9),
        "adapter_down": bell_draw(key_of[7], (D, RANK), D ** -0.5, 0.125),
        "adapter_up": bell_draw(key_of[8], (RANK, FF), RANK ** -0.5, 0.5, ((1, 256),)),
        "gate_weight": bell_draw(key_of[9], (D, FF), D ** -0.5, 0.125, ((1, 256),)),
        "up_weight": bell_draw(key_of[10], (D, FF), D ** -0.5, 0.125, ((1, 256),)),
        "down_weight": bell_draw(key_of[11], (FF, D), FF ** -0.5, 0.09375, ((0, 256),)),
        "row_order": jax.vmap(lambda own: jax.random.permutation(own, CAP))(jax.random.split(key_of[12], N_REQ)).reshape((N_REQ, CAP)).astype(jnp.int32),
        "block_table": jax.vmap(lambda own: jax.random.permutation(own, NB))(jax.random.split(key_of[13], N_REQ)).reshape((N_REQ, NB)).astype(jnp.int32),
    }


def matmul_f32(left, right):
    return jnp.dot(left.astype(jnp.float32), right.astype(jnp.float32), precision=lax.Precision.HIGHEST, preferred_element_type=jnp.float32)

def attend(query_rows, key_rows, value_rows, segment):
    row_count = query_rows.shape[0]
    head_count = query_rows.shape[1] // HD
    query_heads = query_rows.reshape(row_count, head_count, HD).astype(jnp.float32)
    key_heads = key_rows.reshape(row_count, head_count, HD).astype(jnp.float32)
    value_heads = value_rows.reshape(row_count, head_count, HD).astype(jnp.float32)
    scores = jnp.einsum('qhd,khd->hqk', query_heads, key_heads, precision=lax.Precision.HIGHEST) * HD ** (-0.5)
    position = jnp.arange(row_count)
    allowed = (segment[:, None] == segment[None, :]) & (position[None, :] <= position[:, None]) & (segment[:, None] >= 0)
    masked = jnp.where(allowed[None], scores, -1e+30)
    highest = lax.optimization_barrier(jnp.max(masked, axis=-1, keepdims=True))
    exponent = jnp.where(allowed[None], jnp.exp(masked - highest), 0.0)
    denominator = lax.optimization_barrier(jnp.sum(exponent, axis=-1, keepdims=True))
    denominator = jnp.where(denominator > 0, denominator, 1.0)
    weights = (exponent / denominator).astype(jnp.bfloat16)
    result = jnp.einsum('hqk,khd->qhd', weights.astype(jnp.float32), value_heads, precision=lax.Precision.HIGHEST)
    return result.astype(jnp.bfloat16).reshape(row_count, head_count * HD)

def reference(queries, keys, values, resid, seg_ids, out_weight, norm_gain, adapter_down, adapter_up, gate_weight, up_weight, down_weight, row_order, block_table):
    features = HEADS * HD
    query_dev = queries.reshape(N_REQ, CAP, features)
    key_dev = keys.reshape(N_REQ, CAP, features)
    value_dev = values.reshape(N_REQ, CAP, features)
    segment_dev = seg_ids.reshape(N_REQ, CAP)
    attn = lax.map(lambda parts: attend(parts[0], parts[1], parts[2], parts[3]), (query_dev, key_dev, value_dev, segment_dev))
    attn = attn.reshape(N_REQ * CAP, features)
    group_width = features // N_DEC
    summed = jnp.zeros((N_REQ * CAP, D), jnp.float32)
    for group in range(N_DEC):
        partial_value = matmul_f32(attn[:, group * group_width:(group + 1) * group_width], out_weight[group * group_width:(group + 1) * group_width]).astype(jnp.bfloat16)
        partial_value = lax.optimization_barrier(partial_value)
        summed = summed + partial_value.astype(jnp.float32)
    hidden = (resid.astype(jnp.float32) + summed).astype(jnp.bfloat16)
    per_group = CAP // N_REQ
    hidden_dev = hidden.reshape(N_REQ, CAP, D)
    permuted = jax.vmap(lambda rows, order: rows[order])(hidden_dev, row_order)
    mixed = permuted.reshape(N_REQ, N_REQ, per_group, D).transpose(1, 0, 2, 3).reshape(N_REQ * CAP, D)
    piece_width = FF // (N_REQ * N_DEC)
    unit_groups = []
    for group in range(N_DEC):
        index = ((np.arange(N_REQ)[:, None] * N_DEC + group) * piece_width + np.arange(piece_width)[None, :]).reshape(-1)
        unit_groups.append(jnp.asarray(index, dtype=jnp.int32))

    def feed_forward(rows):
        values_f = rows.astype(jnp.float32)
        scale = lax.rsqrt(lax.optimization_barrier(jnp.mean(values_f * values_f, axis=-1, keepdims=True)) + 1e-05)
        normed = (values_f * scale * norm_gain).astype(jnp.bfloat16)
        low_rank = matmul_f32(normed, adapter_down).astype(jnp.bfloat16)
        gate = matmul_f32(normed, gate_weight) + matmul_f32(low_rank, adapter_up)
        up_value = matmul_f32(normed, up_weight)
        inner = (jax.nn.gelu(gate) * up_value).astype(jnp.bfloat16)
        total = jnp.zeros((rows.shape[0], D), jnp.float32)
        for group in range(N_DEC):
            index = unit_groups[group]
            down_part = matmul_f32(inner[:, index], down_weight[index]).astype(jnp.bfloat16)
            down_part = lax.optimization_barrier(down_part)
            total = total + down_part.astype(jnp.float32)
        return (values_f + total).astype(jnp.bfloat16)
    block_out = lax.map(feed_forward, mixed.reshape(N_REQ, CAP, D)).reshape(N_REQ * CAP, D)
    inverse = jax.vmap(jnp.argsort)(block_table).astype(jnp.int32)
    key_blocks = keys.reshape(N_REQ, NB, BLK, features)
    value_blocks = values.reshape(N_REQ, NB, BLK, features)
    key_cache = jax.vmap(lambda blocks, order: blocks[order])(key_blocks, inverse)
    value_cache = jax.vmap(lambda blocks, order: blocks[order])(value_blocks, inverse)
    kv_cache = jnp.concatenate([key_cache, value_cache], axis=-1).reshape(N_REQ * NB, BLK, 2 * features)
    return (block_out, kv_cache)
```

```python
import jax
import jax.numpy as jnp
from jax import lax
from jax.sharding import PartitionSpec as P

HD = 128


def attend(query_rows, key_rows, value_rows, segment):
    row_count = query_rows.shape[0]
    head_count = query_rows.shape[1] // HD
    query_heads = query_rows.reshape(row_count, head_count, HD)
    key_heads = key_rows.reshape(row_count, head_count, HD)
    value_heads = value_rows.reshape(row_count, head_count, HD)
    scores = jnp.einsum(
        "qhd,khd->hqk", query_heads, key_heads, preferred_element_type=jnp.float32
    ) * HD ** (-0.5)
    position = jnp.arange(row_count)
    allowed = (
        (segment[:, None] == segment[None, :])
        & (position[None, :] <= position[:, None])
        & (segment[:, None] >= 0)
    )
    masked = jnp.where(allowed[None], scores, -1e30)
    highest = jnp.max(masked, axis=-1, keepdims=True)
    exponent = jnp.where(allowed[None], jnp.exp(masked - highest), 0.0)
    denominator = jnp.sum(exponent, axis=-1, keepdims=True)
    denominator = jnp.where(denominator > 0, denominator, 1.0)
    weights = (exponent / denominator).astype(jnp.bfloat16)
    result = jnp.einsum("hqk,khd->qhd", weights, value_heads, preferred_element_type=jnp.float32)
    return result.astype(jnp.bfloat16).reshape(row_count, head_count * HD)


def reduce_over_dec(part, dec_count):
    rows = part.shape[0]
    quarter = part.shape[1] // dec_count
    pieces = part.reshape(rows, dec_count, quarter).transpose(1, 0, 2)
    got = lax.all_to_all(pieces, "dec", split_axis=0, concat_axis=0, tiled=True)
    return jnp.sum(got.astype(jnp.float32), axis=0)


def body(
    queries,
    keys,
    values,
    resid,
    seg_ids,
    out_weight,
    norm_gain,
    adapter_down,
    adapter_up,
    gate_weight,
    up_weight,
    down_weight,
    row_order,
    block_table,
):
    dec_count = out_weight.shape[1] // out_weight.shape[0]
    features = keys.shape[1]
    quarter = resid.shape[1]
    model_width = down_weight.shape[1]

    gate_up_local = jnp.stack([gate_weight.T, up_weight.T])
    gate_up = lax.all_gather(gate_up_local, "req", axis=1, tiled=True)
    down_adapter_local = jnp.concatenate([down_weight, adapter_up.T], axis=1)
    down_adapter = lax.all_gather(down_adapter_local, "req", axis=0, tiled=True)

    slot_count = keys.shape[0]
    block_count = block_table.shape[1]
    block_slots = slot_count // block_count
    table_row = block_table[0]
    placement = (jnp.arange(block_count)[:, None] == table_row[None, :]).astype(jnp.bfloat16)
    both = jnp.stack(
        [
            keys.reshape(block_count, block_slots, features),
            values.reshape(block_count, block_slots, features),
        ],
        axis=2,
    )
    ordered = jnp.einsum(
        "tj,jbkw->tbkw", placement, both, preferred_element_type=jnp.float32
    ).astype(jnp.bfloat16)
    per_dev = block_count // dec_count
    ordered = ordered.reshape(dec_count, per_dev, block_slots, 2, features)
    moved = lax.all_to_all(ordered, "dec", split_axis=0, concat_axis=0, tiled=True)
    kv_cache = moved.transpose(1, 2, 3, 0, 4).reshape(per_dev, block_slots, 2 * dec_count * features)

    attn = attend(queries, keys, values, seg_ids)
    partial_value = jnp.dot(attn, out_weight, preferred_element_type=jnp.float32).astype(
        jnp.bfloat16
    )
    head_total = reduce_over_dec(partial_value, dec_count)
    hidden = (resid.astype(jnp.float32) + head_total).astype(jnp.bfloat16)

    permuted = jnp.take(hidden, row_order[0], axis=0)
    cap = permuted.shape[0]
    req_n = gate_up.shape[1] // gate_weight.shape[1]
    per_group = cap // req_n
    column = lax.all_to_all(
        permuted.reshape(req_n, per_group, quarter), "req", split_axis=0, concat_axis=0, tiled=True
    ).reshape(cap, quarter)
    spread = jnp.broadcast_to(column[None], (dec_count, cap, quarter))
    quarters = lax.all_to_all(spread, "dec", split_axis=0, concat_axis=0, tiled=True)
    mixed_rows = quarters.transpose(1, 0, 2).reshape(cap, dec_count * quarter)

    values_f = mixed_rows.astype(jnp.float32)
    scale = lax.rsqrt(jnp.mean(values_f * values_f, axis=-1, keepdims=True) + 1e-05)
    normed = (values_f * scale * norm_gain).astype(jnp.bfloat16)
    low_rank = jnp.dot(normed, adapter_down, preferred_element_type=jnp.float32).astype(
        jnp.bfloat16
    )
    contract = (((1,), (1,)), ((), ()))
    gate = lax.dot_general(
        normed, gate_up[0], contract, preferred_element_type=jnp.float32
    ) + lax.dot_general(
        low_rank, down_adapter[:, model_width:], contract, preferred_element_type=jnp.float32
    )
    up = lax.dot_general(normed, gate_up[1], contract, preferred_element_type=jnp.float32)
    hidden_units = (jax.nn.gelu(gate) * up).astype(jnp.bfloat16)
    down_part = jnp.dot(
        hidden_units, down_adapter[:, :model_width], preferred_element_type=jnp.float32
    ).astype(jnp.bfloat16)
    mlp_total = reduce_over_dec(down_part, dec_count)
    block_out = (column.astype(jnp.float32) + mlp_total).astype(jnp.bfloat16)
    return (block_out, kv_cache)


def solution(mesh):
    placed = (
        P("req", "dec"),
        P("req", "dec"),
        P("req", "dec"),
        P("req", "dec"),
        P("req"),
        P("dec", None),
        P(),
        P(),
        P(None, ("req", "dec")),
        P(None, ("req", "dec")),
        P(None, ("req", "dec")),
        P(("req", "dec"), None),
        P("req", None),
        P("req", None),
    )
    return jax.shard_map(
        body,
        mesh=mesh,
        in_specs=placed,
        out_specs=(P("req", "dec"), P(("req", "dec"), None, None)),
        check_vma=False,
    )
```

```python
import jax
import jax.numpy as jnp
from jax import lax
from jax.sharding import PartitionSpec as P

HD = 128


def attend(query_rows, key_rows, value_rows, segment):
    row_count = query_rows.shape[0]
    head_count = query_rows.shape[1] // HD
    query_heads = query_rows.reshape(row_count, head_count, HD)
    key_heads = key_rows.reshape(row_count, head_count, HD)
    value_heads = value_rows.reshape(row_count, head_count, HD)
    scores = jnp.einsum(
        "qhd,khd->hqk", query_heads, key_heads, preferred_element_type=jnp.float32
    ) * HD ** (-0.5)
    position = jnp.arange(row_count)
    allowed = (
        (segment[:, None] == segment[None, :])
        & (position[None, :] <= position[:, None])
        & (segment[:, None] >= 0)
    )
    masked = jnp.where(allowed[None], scores, -1e30)
    highest = jnp.max(masked, axis=-1, keepdims=True)
    exponent = jnp.where(allowed[None], jnp.exp(masked - highest), 0.0)
    denominator = jnp.sum(exponent, axis=-1, keepdims=True)
    denominator = jnp.where(denominator > 0, denominator, 1.0)
    weights = (exponent / denominator).astype(jnp.bfloat16)
    result = jnp.einsum("hqk,khd->qhd", weights, value_heads, preferred_element_type=jnp.float32)
    return result.astype(jnp.bfloat16).reshape(row_count, head_count * HD)


def reduce_over_dec(part, dec_count):
    rows = part.shape[0]
    quarter = part.shape[1] // dec_count
    pieces = part.reshape(rows, dec_count, quarter).transpose(1, 0, 2)
    got = lax.all_to_all(pieces, "dec", split_axis=0, concat_axis=0, tiled=True)
    return jnp.sum(got.astype(jnp.float32), axis=0)


def body(
    queries,
    keys,
    values,
    resid,
    seg_ids,
    out_weight,
    norm_gain,
    adapter_down,
    adapter_up,
    gate_weight,
    up_weight,
    down_weight,
    row_order,
    block_table,
):
    dec_count = out_weight.shape[1] // out_weight.shape[0]
    features = keys.shape[1]
    quarter = resid.shape[1]
    model_width = down_weight.shape[1]

    hidden_width = gate_weight.shape[0]
    unit_rows_local = jnp.concatenate(
        [gate_weight.T, up_weight.T, down_weight, adapter_up.T], axis=1
    )
    unit_rows = lax.all_gather(unit_rows_local, "req", axis=0, tiled=True)
    gate_rows = unit_rows[:, :hidden_width]
    up_rows = unit_rows[:, hidden_width : 2 * hidden_width]
    down_rows = unit_rows[:, 2 * hidden_width : 2 * hidden_width + model_width]
    adapter_rows = unit_rows[:, 2 * hidden_width + model_width :]

    slot_count = keys.shape[0]
    block_count = block_table.shape[1]
    block_slots = slot_count // block_count
    table_row = block_table[0]
    placement = (jnp.arange(block_count)[:, None] == table_row[None, :]).astype(jnp.bfloat16)
    both = jnp.stack(
        [
            keys.reshape(block_count, block_slots, features),
            values.reshape(block_count, block_slots, features),
        ],
        axis=2,
    )
    ordered = jnp.einsum(
        "tj,jbkw->tbkw", placement, both, preferred_element_type=jnp.float32
    ).astype(jnp.bfloat16)
    per_dev = block_count // dec_count
    ordered = ordered.reshape(dec_count, per_dev, block_slots, 2, features)
    moved = lax.all_to_all(ordered, "dec", split_axis=0, concat_axis=0, tiled=True)
    kv_cache = moved.transpose(1, 2, 3, 0, 4).reshape(per_dev, block_slots, 2 * dec_count * features)

    attn = attend(queries, keys, values, seg_ids)
    partial_value = jnp.dot(attn, out_weight, preferred_element_type=jnp.float32).astype(
        jnp.bfloat16
    )
    head_total = reduce_over_dec(partial_value, dec_count)
    hidden = (resid.astype(jnp.float32) + head_total).astype(jnp.bfloat16)

    permuted = jnp.take(hidden, row_order[0], axis=0)
    cap = permuted.shape[0]
    req_n = unit_rows.shape[0] // gate_weight.shape[1]
    per_group = cap // req_n
    column = lax.all_to_all(
        permuted.reshape(req_n, per_group, quarter), "req", split_axis=0, concat_axis=0, tiled=True
    ).reshape(cap, quarter)
    spread = jnp.broadcast_to(column[None], (dec_count, cap, quarter))
    quarters = lax.all_to_all(spread, "dec", split_axis=0, concat_axis=0, tiled=True)
    mixed_rows = quarters.transpose(1, 0, 2).reshape(cap, dec_count * quarter)

    values_f = mixed_rows.astype(jnp.float32)
    scale = lax.rsqrt(jnp.mean(values_f * values_f, axis=-1, keepdims=True) + 1e-05)
    normed = (values_f * scale * norm_gain).astype(jnp.bfloat16)
    low_rank = jnp.dot(normed, adapter_down, preferred_element_type=jnp.float32).astype(
        jnp.bfloat16
    )
    contract = (((1,), (1,)), ((), ()))
    gate = lax.dot_general(
        normed, gate_rows, contract, preferred_element_type=jnp.float32
    ) + lax.dot_general(
        low_rank, adapter_rows, contract, preferred_element_type=jnp.float32
    )
    up = lax.dot_general(normed, up_rows, contract, preferred_element_type=jnp.float32)
    hidden_units = (jax.nn.gelu(gate) * up).astype(jnp.bfloat16)
    down_part = jnp.dot(
        hidden_units, down_rows, preferred_element_type=jnp.float32
    ).astype(jnp.bfloat16)
    mlp_total = reduce_over_dec(down_part, dec_count)
    block_out = (column.astype(jnp.float32) + mlp_total).astype(jnp.bfloat16)
    return (block_out, kv_cache)


def solution(mesh):
    placed = (
        P("req", "dec"),
        P("req", "dec"),
        P("req", "dec"),
        P("req", "dec"),
        P("req"),
        P("dec", None),
        P(),
        P(),
        P(None, ("req", "dec")),
        P(None, ("req", "dec")),
        P(None, ("req", "dec")),
        P(("req", "dec"), None),
        P("req", None),
        P("req", None),
    )
    return jax.shard_map(
        body,
        mesh=mesh,
        in_specs=placed,
        out_specs=(P("req", "dec"), P(("req", "dec"), None, None)),
        check_vma=False,
    )
```

```python
import jax
import jax.numpy as jnp
from jax import lax
from jax.sharding import PartitionSpec as P

HD = 128


def attend(query_rows, key_rows, value_rows, segment):
    row_count = query_rows.shape[0]
    head_count = query_rows.shape[1] // HD
    query_heads = query_rows.reshape(row_count, head_count, HD)
    key_heads = key_rows.reshape(row_count, head_count, HD)
    value_heads = value_rows.reshape(row_count, head_count, HD)
    scores = jnp.einsum(
        "qhd,khd->hqk", query_heads, key_heads, preferred_element_type=jnp.float32
    ) * HD ** (-0.5)
    position = jnp.arange(row_count)
    allowed = (
        (segment[:, None] == segment[None, :])
        & (position[None, :] <= position[:, None])
        & (segment[:, None] >= 0)
    )
    masked = jnp.where(allowed[None], scores, -1e30)
    highest = jnp.max(masked, axis=-1, keepdims=True)
    exponent = jnp.where(allowed[None], jnp.exp(masked - highest), 0.0)
    denominator = jnp.sum(exponent, axis=-1, keepdims=True)
    denominator = jnp.where(denominator > 0, denominator, 1.0)
    weights = (exponent / denominator).astype(jnp.bfloat16)
    result = jnp.einsum("hqk,khd->qhd", weights, value_heads, preferred_element_type=jnp.float32)
    return result.astype(jnp.bfloat16).reshape(row_count, head_count * HD)


def reduce_over_dec(part, dec_count):
    rows = part.shape[0]
    quarter = part.shape[1] // dec_count
    pieces = part.reshape(rows, dec_count, quarter).transpose(1, 0, 2)
    got = lax.all_to_all(pieces, "dec", split_axis=0, concat_axis=0, tiled=True)
    return jnp.sum(got.astype(jnp.float32), axis=0)


def body(
    queries,
    keys,
    values,
    resid,
    seg_ids,
    out_weight,
    norm_gain,
    adapter_down,
    adapter_up,
    gate_weight,
    up_weight,
    down_weight,
    row_order,
    block_table,
):
    dec_count = out_weight.shape[1] // out_weight.shape[0]
    features = keys.shape[1]
    quarter = resid.shape[1]
    model_width = down_weight.shape[1]

    hidden_width = gate_weight.shape[0]
    unit_rows_local = jnp.concatenate(
        [gate_weight.T, up_weight.T, down_weight, adapter_up.T], axis=1
    )
    unit_rows = lax.all_gather(unit_rows_local, "req", axis=0, tiled=True)
    gate_rows = unit_rows[:, :hidden_width]
    up_rows = unit_rows[:, hidden_width : 2 * hidden_width]
    down_rows = unit_rows[:, 2 * hidden_width : 2 * hidden_width + model_width]
    adapter_rows = unit_rows[:, 2 * hidden_width + model_width :]

    slot_count = keys.shape[0]
    block_count = block_table.shape[1]
    block_slots = slot_count // block_count
    table_row = block_table[0]
    placement = (jnp.arange(block_count)[:, None] == table_row[None, :]).astype(jnp.bfloat16)
    both = jnp.stack(
        [
            keys.reshape(block_count, block_slots, features),
            values.reshape(block_count, block_slots, features),
        ],
        axis=2,
    )
    ordered = jnp.einsum(
        "tj,jbkw->tbkw", placement, both, preferred_element_type=jnp.float32
    ).astype(jnp.bfloat16)
    per_dev = block_count // dec_count
    ordered = ordered.reshape(dec_count, per_dev, block_slots, 2, features)
    moved = lax.all_to_all(ordered, "dec", split_axis=0, concat_axis=0, tiled=True)
    kv_cache = moved.transpose(1, 2, 3, 0, 4).reshape(per_dev, block_slots, 2 * dec_count * features)

    attn = attend(queries, keys, values, seg_ids)
    partial_value = jnp.dot(attn, out_weight, preferred_element_type=jnp.float32).astype(
        jnp.bfloat16
    )
    order = row_order[0]
    cap = resid.shape[0]
    req_n = unit_rows.shape[0] // gate_weight.shape[1]
    per_group = cap // req_n
    chunks = 2
    per_chunk = per_group // chunks
    partial_sorted = jnp.take(partial_value, order, axis=0).reshape(
        req_n, chunks, per_chunk, dec_count * quarter
    )
    resid_sorted = jnp.take(resid, order, axis=0).reshape(req_n, chunks, per_chunk, quarter)
    contract = (((1,), (1,)), ((), ()))
    outs = []
    for c in range(chunks):
        rows_c = req_n * per_chunk
        head_total = reduce_over_dec(partial_sorted[:, c].reshape(rows_c, dec_count * quarter), dec_count)
        hidden = (resid_sorted[:, c].reshape(rows_c, quarter).astype(jnp.float32) + head_total).astype(
            jnp.bfloat16
        )
        column = lax.all_to_all(
            hidden.reshape(req_n, per_chunk, quarter), "req", split_axis=0, concat_axis=0, tiled=True
        ).reshape(rows_c, quarter)
        spread = jnp.broadcast_to(column[None], (dec_count, rows_c, quarter))
        quarters = lax.all_to_all(spread, "dec", split_axis=0, concat_axis=0, tiled=True)
        mixed_rows = quarters.transpose(1, 0, 2).reshape(rows_c, dec_count * quarter)

        values_f = mixed_rows.astype(jnp.float32)
        scale = lax.rsqrt(jnp.mean(values_f * values_f, axis=-1, keepdims=True) + 1e-05)
        normed = (values_f * scale * norm_gain).astype(jnp.bfloat16)
        low_rank = jnp.dot(normed, adapter_down, preferred_element_type=jnp.float32).astype(
            jnp.bfloat16
        )
        gate = lax.dot_general(
            normed, gate_rows, contract, preferred_element_type=jnp.float32
        ) + lax.dot_general(low_rank, adapter_rows, contract, preferred_element_type=jnp.float32)
        up = lax.dot_general(normed, up_rows, contract, preferred_element_type=jnp.float32)
        hidden_units = (jax.nn.gelu(gate) * up).astype(jnp.bfloat16)
        down_part = jnp.dot(hidden_units, down_rows, preferred_element_type=jnp.float32).astype(
            jnp.bfloat16
        )
        mlp_total = reduce_over_dec(down_part, dec_count)
        out_c = (column.astype(jnp.float32) + mlp_total).astype(jnp.bfloat16)
        outs.append(out_c.reshape(req_n, per_chunk, quarter))
    block_out = jnp.stack(outs, axis=1).reshape(cap, quarter)
    return (block_out, kv_cache)


def solution(mesh):
    placed = (
        P("req", "dec"),
        P("req", "dec"),
        P("req", "dec"),
        P("req", "dec"),
        P("req"),
        P("dec", None),
        P(),
        P(),
        P(None, ("req", "dec")),
        P(None, ("req", "dec")),
        P(None, ("req", "dec")),
        P(("req", "dec"), None),
        P("req", None),
        P("req", None),
    )
    return jax.shard_map(
        body,
        mesh=mesh,
        in_specs=placed,
        out_specs=(P("req", "dec"), P(("req", "dec"), None, None)),
        check_vma=False,
    )
```

```python
import jax
import jax.numpy as jnp
from jax import lax
from jax.sharding import PartitionSpec as P

HD = 128
REQ = ("req_hi", "core")


def attend(query_rows, key_rows, value_rows, segment):
    row_count = query_rows.shape[0]
    head_count = query_rows.shape[1] // HD
    query_heads = query_rows.reshape(row_count, head_count, HD)
    key_heads = key_rows.reshape(row_count, head_count, HD)
    value_heads = value_rows.reshape(row_count, head_count, HD)
    scores = jnp.einsum(
        "qhd,khd->hqk", query_heads, key_heads, preferred_element_type=jnp.float32
    ) * HD ** (-0.5)
    position = jnp.arange(row_count)
    allowed = (
        (segment[:, None] == segment[None, :])
        & (position[None, :] <= position[:, None])
        & (segment[:, None] >= 0)
    )
    masked = jnp.where(allowed[None], scores, -1e30)
    highest = jnp.max(masked, axis=-1, keepdims=True)
    exponent = jnp.where(allowed[None], jnp.exp(masked - highest), 0.0)
    denominator = jnp.sum(exponent, axis=-1, keepdims=True)
    denominator = jnp.where(denominator > 0, denominator, 1.0)
    weights = (exponent / denominator).astype(jnp.bfloat16)
    result = jnp.einsum("hqk,khd->qhd", weights, value_heads, preferred_element_type=jnp.float32)
    return result.astype(jnp.bfloat16).reshape(row_count, head_count * HD)


def reduce_over_dec(part, dec_count):
    rows = part.shape[0]
    quarter = part.shape[1] // dec_count
    pieces = part.reshape(rows, dec_count, quarter).transpose(1, 0, 2)
    got = lax.all_to_all(pieces, "dec", split_axis=0, concat_axis=0, tiled=True)
    return jnp.sum(got.astype(jnp.float32), axis=0)


def body(
    queries,
    keys,
    values,
    resid,
    seg_ids,
    out_weight,
    norm_gain,
    adapter_down,
    adapter_up,
    gate_weight,
    up_weight,
    down_weight,
    row_order,
    block_table,
):
    dec_count = out_weight.shape[1] // out_weight.shape[0]
    features = keys.shape[1]
    quarter = resid.shape[1]
    model_width = down_weight.shape[1]

    hidden_width = gate_weight.shape[0]
    unit_rows_local = jnp.concatenate(
        [gate_weight.T, up_weight.T, down_weight, adapter_up.T], axis=1
    )
    same_core = lax.all_gather(unit_rows_local, "req_hi", axis=0, tiled=True)
    other_core = lax.ppermute(same_core, "core", [(0, 1), (1, 0)])
    unit_rows = jnp.concatenate([same_core, other_core], axis=0)
    gate_rows = unit_rows[:, :hidden_width]
    up_rows = unit_rows[:, hidden_width : 2 * hidden_width]
    down_rows = unit_rows[:, 2 * hidden_width : 2 * hidden_width + model_width]
    adapter_rows = unit_rows[:, 2 * hidden_width + model_width :]

    slot_count = keys.shape[0]
    block_count = block_table.shape[1]
    block_slots = slot_count // block_count
    table_row = block_table[0]
    placement = (jnp.arange(block_count)[:, None] == table_row[None, :]).astype(jnp.bfloat16)
    both = jnp.stack(
        [
            keys.reshape(block_count, block_slots, features),
            values.reshape(block_count, block_slots, features),
        ],
        axis=2,
    )
    ordered = jnp.einsum(
        "tj,jbkw->tbkw", placement, both, preferred_element_type=jnp.float32
    ).astype(jnp.bfloat16)
    per_dev = block_count // dec_count
    ordered = ordered.reshape(dec_count, per_dev, block_slots, 2, features)
    moved = lax.all_to_all(ordered, "dec", split_axis=0, concat_axis=0, tiled=True)
    kv_cache = moved.transpose(1, 2, 3, 0, 4).reshape(per_dev, block_slots, 2 * dec_count * features)

    attn = attend(queries, keys, values, seg_ids)
    partial_value = jnp.dot(attn, out_weight, preferred_element_type=jnp.float32).astype(
        jnp.bfloat16
    )
    head_total = reduce_over_dec(partial_value, dec_count)
    hidden = (resid.astype(jnp.float32) + head_total).astype(jnp.bfloat16)

    permuted = jnp.take(hidden, row_order[0], axis=0)
    cap = permuted.shape[0]
    req_n = unit_rows.shape[0] // gate_weight.shape[1]
    per_group = cap // req_n
    column = lax.all_to_all(
        permuted.reshape(req_n, per_group, quarter), REQ, split_axis=0, concat_axis=0, tiled=True
    ).reshape(cap, quarter)
    spread = jnp.broadcast_to(column[None], (dec_count, cap, quarter))
    quarters = lax.all_to_all(spread, "dec", split_axis=0, concat_axis=0, tiled=True)
    mixed_rows = quarters.transpose(1, 0, 2).reshape(cap, dec_count * quarter)

    values_f = mixed_rows.astype(jnp.float32)
    scale = lax.rsqrt(jnp.mean(values_f * values_f, axis=-1, keepdims=True) + 1e-05)
    normed = (values_f * scale * norm_gain).astype(jnp.bfloat16)
    low_rank = jnp.dot(normed, adapter_down, preferred_element_type=jnp.float32).astype(
        jnp.bfloat16
    )
    contract = (((1,), (1,)), ((), ()))
    gate = lax.dot_general(
        normed, gate_rows, contract, preferred_element_type=jnp.float32
    ) + lax.dot_general(
        low_rank, adapter_rows, contract, preferred_element_type=jnp.float32
    )
    up = lax.dot_general(normed, up_rows, contract, preferred_element_type=jnp.float32)
    hidden_units = (jax.nn.gelu(gate) * up).astype(jnp.bfloat16)
    down_part = jnp.dot(
        hidden_units, down_rows, preferred_element_type=jnp.float32
    ).astype(jnp.bfloat16)
    mlp_total = reduce_over_dec(down_part, dec_count)
    block_out = (column.astype(jnp.float32) + mlp_total).astype(jnp.bfloat16)
    return (block_out, kv_cache)


def solution(mesh):
    req_size = mesh.shape["req"]
    split = jax.sharding.Mesh(
        mesh.devices.reshape(req_size // 2, 2, mesh.shape["dec"]), ("req_hi", "core", "dec")
    )
    placed = (
        P(REQ, "dec"),
        P(REQ, "dec"),
        P(REQ, "dec"),
        P(REQ, "dec"),
        P(REQ),
        P("dec", None),
        P(),
        P(),
        P(None, (*REQ, "dec")),
        P(None, (*REQ, "dec")),
        P(None, (*REQ, "dec")),
        P((*REQ, "dec"), None),
        P(REQ, None),
        P(REQ, None),
    )
    return jax.shard_map(
        body,
        mesh=split,
        in_specs=placed,
        out_specs=(P(REQ, "dec"), P((*REQ, "dec"), None, None)),
        check_vma=False,
    )
```

```python
import jax
import jax.numpy as jnp
from jax import lax
from jax.sharding import PartitionSpec as P

HD = 128


def attend(query_rows, key_rows, value_rows, segment):
    row_count = query_rows.shape[0]
    head_count = query_rows.shape[1] // HD
    query_heads = query_rows.reshape(row_count, head_count, HD)
    key_heads = key_rows.reshape(row_count, head_count, HD)
    value_heads = value_rows.reshape(row_count, head_count, HD)
    scores = jnp.einsum(
        "qhd,khd->hqk", query_heads, key_heads, preferred_element_type=jnp.float32
    ) * HD ** (-0.5)
    position = jnp.arange(row_count)
    allowed = (
        (segment[:, None] == segment[None, :])
        & (position[None, :] <= position[:, None])
        & (segment[:, None] >= 0)
    )
    masked = jnp.where(allowed[None], scores, -1e30)
    highest = jnp.max(masked, axis=-1, keepdims=True)
    exponent = jnp.where(allowed[None], jnp.exp(masked - highest), 0.0)
    denominator = jnp.sum(exponent, axis=-1, keepdims=True)
    denominator = jnp.where(denominator > 0, denominator, 1.0)
    weights = (exponent / denominator).astype(jnp.bfloat16)
    result = jnp.einsum("hqk,khd->qhd", weights, value_heads, preferred_element_type=jnp.float32)
    return result.astype(jnp.bfloat16).reshape(row_count, head_count * HD)


def reduce_over_dec(part, dec_count):
    quarter = part.shape[1] // dec_count
    here = lax.axis_index("dec")
    total = lax.dynamic_slice_in_dim(part, here * quarter, quarter, 1).astype(jnp.float32)
    for shift in range(1, dec_count):
        piece = lax.dynamic_slice_in_dim(part, ((here + shift) % dec_count) * quarter, quarter, 1)
        pairs = [(i, (i + shift) % dec_count) for i in range(dec_count)]
        total = total + lax.ppermute(piece, "dec", pairs).astype(jnp.float32)
    return total


def gather_over_dec(column, dec_count):
    here = lax.axis_index("dec")
    arrived = [column]
    for shift in range(1, dec_count):
        pairs = [(i, (i + shift) % dec_count) for i in range(dec_count)]
        arrived.append(lax.ppermute(column, "dec", pairs))
    stacked = jnp.stack(arrived)
    by_quarter = jnp.take(stacked, (here - jnp.arange(dec_count)) % dec_count, axis=0)
    rows = column.shape[0]
    return by_quarter.transpose(1, 0, 2).reshape(rows, dec_count * column.shape[1])


def body(
    queries,
    keys,
    values,
    resid,
    seg_ids,
    out_weight,
    norm_gain,
    adapter_down,
    adapter_up,
    gate_weight,
    up_weight,
    down_weight,
    row_order,
    block_table,
):
    dec_count = out_weight.shape[1] // out_weight.shape[0]
    features = keys.shape[1]
    quarter = resid.shape[1]
    model_width = down_weight.shape[1]

    hidden_width = gate_weight.shape[0]
    unit_rows_local = jnp.concatenate(
        [gate_weight.T, up_weight.T, down_weight, adapter_up.T], axis=1
    )
    unit_rows = lax.all_gather(unit_rows_local, "req", axis=0, tiled=True)
    gate_rows = unit_rows[:, :hidden_width]
    up_rows = unit_rows[:, hidden_width : 2 * hidden_width]
    down_rows = unit_rows[:, 2 * hidden_width : 2 * hidden_width + model_width]
    adapter_rows = unit_rows[:, 2 * hidden_width + model_width :]

    slot_count = keys.shape[0]
    block_count = block_table.shape[1]
    block_slots = slot_count // block_count
    table_row = block_table[0]
    placement = (jnp.arange(block_count)[:, None] == table_row[None, :]).astype(jnp.bfloat16)
    both = jnp.stack(
        [
            keys.reshape(block_count, block_slots, features),
            values.reshape(block_count, block_slots, features),
        ],
        axis=2,
    )
    ordered = jnp.einsum(
        "tj,jbkw->tbkw", placement, both, preferred_element_type=jnp.float32
    ).astype(jnp.bfloat16)
    per_dev = block_count // dec_count
    ordered = ordered.reshape(dec_count, per_dev, block_slots, 2, features)
    moved = lax.all_to_all(ordered, "dec", split_axis=0, concat_axis=0, tiled=True)
    kv_cache = moved.transpose(1, 2, 3, 0, 4).reshape(per_dev, block_slots, 2 * dec_count * features)

    attn = attend(queries, keys, values, seg_ids)
    partial_value = jnp.dot(attn, out_weight, preferred_element_type=jnp.float32).astype(
        jnp.bfloat16
    )
    head_total = reduce_over_dec(partial_value, dec_count)
    hidden = (resid.astype(jnp.float32) + head_total).astype(jnp.bfloat16)

    permuted = jnp.take(hidden, row_order[0], axis=0)
    cap = permuted.shape[0]
    req_n = unit_rows.shape[0] // gate_weight.shape[1]
    per_group = cap // req_n
    column = lax.all_to_all(
        permuted.reshape(req_n, per_group, quarter), "req", split_axis=0, concat_axis=0, tiled=True
    ).reshape(cap, quarter)
    mixed_rows = gather_over_dec(column, dec_count)

    values_f = mixed_rows.astype(jnp.float32)
    scale = lax.rsqrt(jnp.mean(values_f * values_f, axis=-1, keepdims=True) + 1e-05)
    normed = (values_f * scale * norm_gain).astype(jnp.bfloat16)
    low_rank = jnp.dot(normed, adapter_down, preferred_element_type=jnp.float32).astype(
        jnp.bfloat16
    )
    contract = (((1,), (1,)), ((), ()))
    gate = lax.dot_general(
        normed, gate_rows, contract, preferred_element_type=jnp.float32
    ) + lax.dot_general(
        low_rank, adapter_rows, contract, preferred_element_type=jnp.float32
    )
    up = lax.dot_general(normed, up_rows, contract, preferred_element_type=jnp.float32)
    hidden_units = (jax.nn.gelu(gate) * up).astype(jnp.bfloat16)
    down_part = jnp.dot(
        hidden_units, down_rows, preferred_element_type=jnp.float32
    ).astype(jnp.bfloat16)
    mlp_total = reduce_over_dec(down_part, dec_count)
    block_out = (column.astype(jnp.float32) + mlp_total).astype(jnp.bfloat16)
    return (block_out, kv_cache)


def solution(mesh):
    placed = (
        P("req", "dec"),
        P("req", "dec"),
        P("req", "dec"),
        P("req", "dec"),
        P("req"),
        P("dec", None),
        P(),
        P(),
        P(None, ("req", "dec")),
        P(None, ("req", "dec")),
        P(None, ("req", "dec")),
        P(("req", "dec"), None),
        P("req", None),
        P("req", None),
    )
    return jax.shard_map(
        body,
        mesh=mesh,
        in_specs=placed,
        out_specs=(P("req", "dec"), P(("req", "dec"), None, None)),
        check_vma=False,
    )
```

```python
import jax
import jax.numpy as jnp
from jax import lax
from jax.sharding import PartitionSpec as P

HD = 128


def attend(query_rows, key_rows, value_rows, segment):
    row_count = query_rows.shape[0]
    head_count = query_rows.shape[1] // HD
    query_heads = query_rows.reshape(row_count, head_count, HD)
    key_heads = key_rows.reshape(row_count, head_count, HD)
    value_heads = value_rows.reshape(row_count, head_count, HD)
    scores = jnp.einsum(
        "qhd,khd->hqk", query_heads, key_heads, preferred_element_type=jnp.float32
    ) * HD ** (-0.5)
    position = jnp.arange(row_count)
    allowed = (
        (segment[:, None] == segment[None, :])
        & (position[None, :] <= position[:, None])
        & (segment[:, None] >= 0)
    )
    masked = jnp.where(allowed[None], scores, -1e30)
    highest = jnp.max(masked, axis=-1, keepdims=True)
    exponent = jnp.where(allowed[None], jnp.exp(masked - highest), 0.0)
    denominator = jnp.sum(exponent, axis=-1, keepdims=True)
    denominator = jnp.where(denominator > 0, denominator, 1.0)
    weights = (exponent / denominator).astype(jnp.bfloat16)
    result = jnp.einsum("hqk,khd->qhd", weights, value_heads, preferred_element_type=jnp.float32)
    return result.astype(jnp.bfloat16).reshape(row_count, head_count * HD)


def reduce_over_dec(part, dec_count):
    quarter = part.shape[1] // dec_count
    here = lax.axis_index("dec")
    total = lax.dynamic_slice_in_dim(part, here * quarter, quarter, 1).astype(jnp.float32)
    for shift in range(1, dec_count):
        piece = lax.dynamic_slice_in_dim(part, ((here + shift) % dec_count) * quarter, quarter, 1)
        pairs = [(i, (i + shift) % dec_count) for i in range(dec_count)]
        total = total + lax.ppermute(piece, "dec", pairs).astype(jnp.float32)
    return total


def body(
    queries,
    keys,
    values,
    resid,
    seg_ids,
    out_weight,
    norm_gain,
    adapter_down,
    adapter_up,
    gate_weight,
    up_weight,
    down_weight,
    row_order,
    block_table,
):
    dec_count = out_weight.shape[1] // out_weight.shape[0]
    features = keys.shape[1]
    quarter = resid.shape[1]
    model_width = down_weight.shape[1]

    hidden_width = gate_weight.shape[0]
    unit_rows_local = jnp.concatenate(
        [gate_weight.T, up_weight.T, down_weight, adapter_up.T], axis=1
    )
    unit_rows = lax.all_gather(unit_rows_local, "req", axis=0, tiled=True)
    gate_rows = unit_rows[:, :hidden_width]
    up_rows = unit_rows[:, hidden_width : 2 * hidden_width]
    down_rows = unit_rows[:, 2 * hidden_width : 2 * hidden_width + model_width]
    adapter_rows = unit_rows[:, 2 * hidden_width + model_width :]

    slot_count = keys.shape[0]
    block_count = block_table.shape[1]
    block_slots = slot_count // block_count
    table_row = block_table[0]
    placement = (jnp.arange(block_count)[:, None] == table_row[None, :]).astype(jnp.bfloat16)
    both = jnp.stack(
        [
            keys.reshape(block_count, block_slots, features),
            values.reshape(block_count, block_slots, features),
        ],
        axis=2,
    )
    ordered = jnp.einsum(
        "tj,jbkw->tbkw", placement, both, preferred_element_type=jnp.float32
    ).astype(jnp.bfloat16)
    per_dev = block_count // dec_count
    ordered = ordered.reshape(dec_count, per_dev, block_slots, 2, features)

    attn = attend(queries, keys, values, seg_ids)
    partial_value = jnp.dot(attn, out_weight, preferred_element_type=jnp.float32).astype(
        jnp.bfloat16
    )
    head_total = reduce_over_dec(partial_value, dec_count)
    hidden = (resid.astype(jnp.float32) + head_total).astype(jnp.bfloat16)

    permuted = jnp.take(hidden, row_order[0], axis=0)
    cap = permuted.shape[0]
    req_n = unit_rows.shape[0] // gate_weight.shape[1]
    per_group = cap // req_n
    column = lax.all_to_all(
        permuted.reshape(req_n, per_group, quarter), "req", split_axis=0, concat_axis=0, tiled=True
    ).reshape(cap, quarter)
    spread = jnp.broadcast_to(column[None], (dec_count, cap, quarter))
    quarters = lax.all_to_all(spread, "dec", split_axis=0, concat_axis=0, tiled=True)
    mixed_rows = quarters.transpose(1, 0, 2).reshape(cap, dec_count * quarter)
    mixed_rows, ordered = lax.optimization_barrier((mixed_rows, ordered))
    moved = lax.all_to_all(ordered, "dec", split_axis=0, concat_axis=0, tiled=True)
    kv_cache = moved.transpose(1, 2, 3, 0, 4).reshape(per_dev, block_slots, 2 * dec_count * features)

    values_f = mixed_rows.astype(jnp.float32)
    scale = lax.rsqrt(jnp.mean(values_f * values_f, axis=-1, keepdims=True) + 1e-05)
    normed = (values_f * scale * norm_gain).astype(jnp.bfloat16)
    low_rank = jnp.dot(normed, adapter_down, preferred_element_type=jnp.float32).astype(
        jnp.bfloat16
    )
    contract = (((1,), (1,)), ((), ()))
    gate = lax.dot_general(
        normed, gate_rows, contract, preferred_element_type=jnp.float32
    ) + lax.dot_general(
        low_rank, adapter_rows, contract, preferred_element_type=jnp.float32
    )
    up = lax.dot_general(normed, up_rows, contract, preferred_element_type=jnp.float32)
    hidden_units = (jax.nn.gelu(gate) * up).astype(jnp.bfloat16)
    down_part = jnp.dot(
        hidden_units, down_rows, preferred_element_type=jnp.float32
    ).astype(jnp.bfloat16)
    mlp_total = reduce_over_dec(down_part, dec_count)
    block_out = (column.astype(jnp.float32) + mlp_total).astype(jnp.bfloat16)
    return (block_out, kv_cache)


def solution(mesh):
    placed = (
        P("req", "dec"),
        P("req", "dec"),
        P("req", "dec"),
        P("req", "dec"),
        P("req"),
        P("dec", None),
        P(),
        P(),
        P(None, ("req", "dec")),
        P(None, ("req", "dec")),
        P(None, ("req", "dec")),
        P(("req", "dec"), None),
        P("req", None),
        P("req", None),
    )
    return jax.shard_map(
        body,
        mesh=mesh,
        in_specs=placed,
        out_specs=(P("req", "dec"), P(("req", "dec"), None, None)),
        check_vma=False,
    )
```

```python
import jax
import jax.numpy as jnp
from jax import lax
from jax.sharding import PartitionSpec as P

HD = 128


def attend(query_rows, key_rows, value_rows, segment):
    row_count = query_rows.shape[0]
    head_count = query_rows.shape[1] // HD
    query_heads = query_rows.reshape(row_count, head_count, HD)
    key_heads = key_rows.reshape(row_count, head_count, HD)
    value_heads = value_rows.reshape(row_count, head_count, HD)
    scores = jnp.einsum(
        "qhd,khd->hqk", query_heads, key_heads, preferred_element_type=jnp.float32
    ) * HD ** (-0.5)
    position = jnp.arange(row_count)
    allowed = (
        (segment[:, None] == segment[None, :])
        & (position[None, :] <= position[:, None])
        & (segment[:, None] >= 0)
    )
    masked = jnp.where(allowed[None], scores, -1e30)
    highest = jnp.max(masked, axis=-1, keepdims=True)
    exponent = jnp.where(allowed[None], jnp.exp(masked - highest), 0.0)
    denominator = jnp.sum(exponent, axis=-1, keepdims=True)
    denominator = jnp.where(denominator > 0, denominator, 1.0)
    weights = (exponent / denominator).astype(jnp.bfloat16)
    result = jnp.einsum("hqk,khd->qhd", weights, value_heads, preferred_element_type=jnp.float32)
    return result.astype(jnp.bfloat16).reshape(row_count, head_count * HD)


def reduce_over_dec(part, dec_count):
    quarter = part.shape[1] // dec_count
    here = lax.axis_index("dec")
    total = lax.dynamic_slice_in_dim(part, here * quarter, quarter, 1).astype(jnp.float32)
    for shift in range(1, dec_count):
        piece = lax.dynamic_slice_in_dim(part, ((here + shift) % dec_count) * quarter, quarter, 1)
        pairs = [(i, (i + shift) % dec_count) for i in range(dec_count)]
        total = total + lax.ppermute(piece, "dec", pairs).astype(jnp.float32)
    return total


def gather_over_dec(column, dec_count):
    here = lax.axis_index("dec")
    arrived = [column]
    for shift in range(1, dec_count):
        pairs = [(i, (i + shift) % dec_count) for i in range(dec_count)]
        arrived.append(lax.ppermute(column, "dec", pairs))
    stacked = jnp.stack(arrived)
    by_quarter = jnp.take(stacked, (here - jnp.arange(dec_count)) % dec_count, axis=0)
    rows = column.shape[0]
    return by_quarter.transpose(1, 0, 2).reshape(rows, dec_count * column.shape[1])


def body(
    queries,
    keys,
    values,
    resid,
    seg_ids,
    out_weight,
    norm_gain,
    adapter_down,
    adapter_up,
    gate_weight,
    up_weight,
    down_weight,
    row_order,
    block_table,
):
    dec_count = out_weight.shape[1] // out_weight.shape[0]
    features = keys.shape[1]
    quarter = resid.shape[1]
    model_width = down_weight.shape[1]

    hidden_width = gate_weight.shape[0]
    unit_rows_local = jnp.concatenate(
        [gate_weight.T, up_weight.T, down_weight, adapter_up.T], axis=1
    )
    unit_rows = lax.all_gather(unit_rows_local, "req", axis=0, tiled=True)
    gate_rows = unit_rows[:, :hidden_width]
    up_rows = unit_rows[:, hidden_width : 2 * hidden_width]
    down_rows = unit_rows[:, 2 * hidden_width : 2 * hidden_width + model_width]
    adapter_rows = unit_rows[:, 2 * hidden_width + model_width :]

    slot_count = keys.shape[0]
    block_count = block_table.shape[1]
    block_slots = slot_count // block_count
    table_row = block_table[0]
    placement = (jnp.arange(block_count)[:, None] == table_row[None, :]).astype(jnp.bfloat16)
    both = jnp.stack(
        [
            keys.reshape(block_count, block_slots, features),
            values.reshape(block_count, block_slots, features),
        ],
        axis=2,
    )
    ordered = jnp.einsum(
        "tj,jbkw->tbkw", placement, both, preferred_element_type=jnp.float32
    ).astype(jnp.bfloat16)
    per_dev = block_count // dec_count
    ordered = ordered.reshape(dec_count, per_dev, block_slots, 2, features)

    attn = attend(queries, keys, values, seg_ids)
    partial_value = jnp.dot(attn, out_weight, preferred_element_type=jnp.float32).astype(
        jnp.bfloat16
    )
    head_total = reduce_over_dec(partial_value, dec_count)
    hidden = (resid.astype(jnp.float32) + head_total).astype(jnp.bfloat16)

    permuted = jnp.take(hidden, row_order[0], axis=0)
    cap = permuted.shape[0]
    req_n = unit_rows.shape[0] // gate_weight.shape[1]
    per_group = cap // req_n
    column = lax.all_to_all(
        permuted.reshape(req_n, per_group, quarter), "req", split_axis=0, concat_axis=0, tiled=True
    ).reshape(cap, quarter)
    mixed_rows = gather_over_dec(column, dec_count)
    mixed_rows, ordered = lax.optimization_barrier((mixed_rows, ordered))
    moved = lax.all_to_all(ordered, "dec", split_axis=0, concat_axis=0, tiled=True)
    kv_cache = moved.transpose(1, 2, 3, 0, 4).reshape(per_dev, block_slots, 2 * dec_count * features)

    values_f = mixed_rows.astype(jnp.float32)
    scale = lax.rsqrt(jnp.mean(values_f * values_f, axis=-1, keepdims=True) + 1e-05)
    normed = (values_f * scale * norm_gain).astype(jnp.bfloat16)
    low_rank = jnp.dot(normed, adapter_down, preferred_element_type=jnp.float32).astype(
        jnp.bfloat16
    )
    contract = (((1,), (1,)), ((), ()))
    gate = lax.dot_general(
        normed, gate_rows, contract, preferred_element_type=jnp.float32
    ) + lax.dot_general(
        low_rank, adapter_rows, contract, preferred_element_type=jnp.float32
    )
    up = lax.dot_general(normed, up_rows, contract, preferred_element_type=jnp.float32)
    hidden_units = (jax.nn.gelu(gate) * up).astype(jnp.bfloat16)
    down_part = jnp.dot(
        hidden_units, down_rows, preferred_element_type=jnp.float32
    ).astype(jnp.bfloat16)
    mlp_total = reduce_over_dec(down_part, dec_count)
    block_out = (column.astype(jnp.float32) + mlp_total).astype(jnp.bfloat16)
    return (block_out, kv_cache)


def solution(mesh):
    placed = (
        P("req", "dec"),
        P("req", "dec"),
        P("req", "dec"),
        P("req", "dec"),
        P("req"),
        P("dec", None),
        P(),
        P(),
        P(None, ("req", "dec")),
        P(None, ("req", "dec")),
        P(None, ("req", "dec")),
        P(("req", "dec"), None),
        P("req", None),
        P("req", None),
    )
    return jax.shard_map(
        body,
        mesh=mesh,
        in_specs=placed,
        out_specs=(P("req", "dec"), P(("req", "dec"), None, None)),
        check_vma=False,
    )
```

```python
import jax
import jax.numpy as jnp
from jax import lax
from jax.sharding import PartitionSpec as P

HD = 128


def attend(query_rows, key_rows, value_rows, segment):
    row_count = query_rows.shape[0]
    head_count = query_rows.shape[1] // HD
    query_heads = query_rows.reshape(row_count, head_count, HD)
    key_heads = key_rows.reshape(row_count, head_count, HD)
    value_heads = value_rows.reshape(row_count, head_count, HD)
    scores = jnp.einsum(
        "qhd,khd->hqk", query_heads, key_heads, preferred_element_type=jnp.float32
    ) * HD ** (-0.5)
    position = jnp.arange(row_count)
    allowed = (
        (segment[:, None] == segment[None, :])
        & (position[None, :] <= position[:, None])
        & (segment[:, None] >= 0)
    )
    masked = jnp.where(allowed[None], scores, -1e30)
    highest = jnp.max(masked, axis=-1, keepdims=True)
    exponent = jnp.where(allowed[None], jnp.exp(masked - highest), 0.0)
    denominator = jnp.sum(exponent, axis=-1, keepdims=True)
    denominator = jnp.where(denominator > 0, denominator, 1.0)
    weights = (exponent / denominator).astype(jnp.bfloat16)
    result = jnp.einsum("hqk,khd->qhd", weights, value_heads, preferred_element_type=jnp.float32)
    return result.astype(jnp.bfloat16).reshape(row_count, head_count * HD)


def project_reduce_over_dec(lhs, rhs, dec_count):
    quarter = rhs.shape[1] // dec_count
    here = lax.axis_index("dec")

    def quarter_of(index):
        block = lax.dynamic_slice_in_dim(rhs, index * quarter, quarter, 1)
        return jnp.dot(lhs, block, preferred_element_type=jnp.float32).astype(jnp.bfloat16)

    arrived = []
    for shift in range(1, dec_count):
        piece = quarter_of((here + shift) % dec_count)
        pairs = [(i, (i + shift) % dec_count) for i in range(dec_count)]
        arrived.append(lax.ppermute(piece, "dec", pairs))
    total = quarter_of(here).astype(jnp.float32)
    for piece in arrived:
        total = total + piece.astype(jnp.float32)
    return total


def body(
    queries,
    keys,
    values,
    resid,
    seg_ids,
    out_weight,
    norm_gain,
    adapter_down,
    adapter_up,
    gate_weight,
    up_weight,
    down_weight,
    row_order,
    block_table,
):
    dec_count = out_weight.shape[1] // out_weight.shape[0]
    features = keys.shape[1]
    quarter = resid.shape[1]
    model_width = down_weight.shape[1]

    hidden_width = gate_weight.shape[0]
    unit_rows_local = jnp.concatenate(
        [gate_weight.T, up_weight.T, down_weight, adapter_up.T], axis=1
    )
    unit_rows = lax.all_gather(unit_rows_local, "req", axis=0, tiled=True)
    gate_rows = unit_rows[:, :hidden_width]
    up_rows = unit_rows[:, hidden_width : 2 * hidden_width]
    down_rows = unit_rows[:, 2 * hidden_width : 2 * hidden_width + model_width]
    adapter_rows = unit_rows[:, 2 * hidden_width + model_width :]

    slot_count = keys.shape[0]
    block_count = block_table.shape[1]
    block_slots = slot_count // block_count
    table_row = block_table[0]
    placement = (jnp.arange(block_count)[:, None] == table_row[None, :]).astype(jnp.bfloat16)
    both = jnp.stack(
        [
            keys.reshape(block_count, block_slots, features),
            values.reshape(block_count, block_slots, features),
        ],
        axis=2,
    )
    ordered = jnp.einsum(
        "tj,jbkw->tbkw", placement, both, preferred_element_type=jnp.float32
    ).astype(jnp.bfloat16)
    per_dev = block_count // dec_count
    ordered = ordered.reshape(dec_count, per_dev, block_slots, 2, features)

    attn = attend(queries, keys, values, seg_ids)
    head_total = project_reduce_over_dec(attn, out_weight, dec_count)
    hidden = (resid.astype(jnp.float32) + head_total).astype(jnp.bfloat16)

    permuted = jnp.take(hidden, row_order[0], axis=0)
    cap = permuted.shape[0]
    req_n = unit_rows.shape[0] // gate_weight.shape[1]
    per_group = cap // req_n
    column = lax.all_to_all(
        permuted.reshape(req_n, per_group, quarter), "req", split_axis=0, concat_axis=0, tiled=True
    ).reshape(cap, quarter)
    spread = jnp.broadcast_to(column[None], (dec_count, cap, quarter))
    quarters = lax.all_to_all(spread, "dec", split_axis=0, concat_axis=0, tiled=True)
    mixed_rows = quarters.transpose(1, 0, 2).reshape(cap, dec_count * quarter)
    mixed_rows, ordered = lax.optimization_barrier((mixed_rows, ordered))
    moved = lax.all_to_all(ordered, "dec", split_axis=0, concat_axis=0, tiled=True)
    kv_cache = moved.transpose(1, 2, 3, 0, 4).reshape(per_dev, block_slots, 2 * dec_count * features)

    values_f = mixed_rows.astype(jnp.float32)
    scale = lax.rsqrt(jnp.mean(values_f * values_f, axis=-1, keepdims=True) + 1e-05)
    normed = (values_f * scale * norm_gain).astype(jnp.bfloat16)
    low_rank = jnp.dot(normed, adapter_down, preferred_element_type=jnp.float32).astype(
        jnp.bfloat16
    )
    contract = (((1,), (1,)), ((), ()))
    gate = lax.dot_general(
        normed, gate_rows, contract, preferred_element_type=jnp.float32
    ) + lax.dot_general(
        low_rank, adapter_rows, contract, preferred_element_type=jnp.float32
    )
    up = lax.dot_general(normed, up_rows, contract, preferred_element_type=jnp.float32)
    hidden_units = (jax.nn.gelu(gate) * up).astype(jnp.bfloat16)
    mlp_total = project_reduce_over_dec(hidden_units, down_rows, dec_count)
    block_out = (column.astype(jnp.float32) + mlp_total).astype(jnp.bfloat16)
    return (block_out, kv_cache)


def solution(mesh):
    placed = (
        P("req", "dec"),
        P("req", "dec"),
        P("req", "dec"),
        P("req", "dec"),
        P("req"),
        P("dec", None),
        P(),
        P(),
        P(None, ("req", "dec")),
        P(None, ("req", "dec")),
        P(None, ("req", "dec")),
        P(("req", "dec"), None),
        P("req", None),
        P("req", None),
    )
    return jax.shard_map(
        body,
        mesh=mesh,
        in_specs=placed,
        out_specs=(P("req", "dec"), P(("req", "dec"), None, None)),
        check_vma=False,
    )
```

```python
import jax
import jax.numpy as jnp
from jax import lax
from jax.sharding import PartitionSpec as P

HD = 128


def attend(query_rows, key_rows, value_rows, segment):
    row_count = query_rows.shape[0]
    head_count = query_rows.shape[1] // HD
    query_heads = query_rows.reshape(row_count, head_count, HD)
    key_heads = key_rows.reshape(row_count, head_count, HD)
    value_heads = value_rows.reshape(row_count, head_count, HD)
    scores = jnp.einsum(
        "qhd,khd->hqk", query_heads, key_heads, preferred_element_type=jnp.float32
    ) * HD ** (-0.5)
    position = jnp.arange(row_count)
    allowed = (
        (segment[:, None] == segment[None, :])
        & (position[None, :] <= position[:, None])
        & (segment[:, None] >= 0)
    )
    masked = jnp.where(allowed[None], scores, -1e30)
    highest = jnp.max(masked, axis=-1, keepdims=True)
    exponent = jnp.where(allowed[None], jnp.exp(masked - highest), 0.0)
    denominator = jnp.sum(exponent, axis=-1, keepdims=True)
    denominator = jnp.where(denominator > 0, denominator, 1.0)
    weights = (exponent / denominator).astype(jnp.bfloat16)
    result = jnp.einsum("hqk,khd->qhd", weights, value_heads, preferred_element_type=jnp.float32)
    return result.astype(jnp.bfloat16).reshape(row_count, head_count * HD)


def project_reduce_over_dec(lhs, rhs, dec_count):
    quarter = rhs.shape[1] // dec_count
    here = lax.axis_index("dec")

    def quarter_of(index):
        block = lax.dynamic_slice_in_dim(rhs, index * quarter, quarter, 1)
        return jnp.dot(lhs, block, preferred_element_type=jnp.float32).astype(jnp.bfloat16)

    arrived = []
    for shift in range(1, dec_count):
        piece = quarter_of((here + shift) % dec_count)
        pairs = [(i, (i + shift) % dec_count) for i in range(dec_count)]
        arrived.append(lax.ppermute(piece, "dec", pairs))
    total = quarter_of(here).astype(jnp.float32)
    for piece in arrived:
        total = total + piece.astype(jnp.float32)
    return total


def reduce_over_dec(part, dec_count):
    quarter = part.shape[1] // dec_count
    here = lax.axis_index("dec")
    total = lax.dynamic_slice_in_dim(part, here * quarter, quarter, 1).astype(jnp.float32)
    for shift in range(1, dec_count):
        piece = lax.dynamic_slice_in_dim(part, ((here + shift) % dec_count) * quarter, quarter, 1)
        pairs = [(i, (i + shift) % dec_count) for i in range(dec_count)]
        total = total + lax.ppermute(piece, "dec", pairs).astype(jnp.float32)
    return total


def body(
    queries,
    keys,
    values,
    resid,
    seg_ids,
    out_weight,
    norm_gain,
    adapter_down,
    adapter_up,
    gate_weight,
    up_weight,
    down_weight,
    row_order,
    block_table,
):
    dec_count = out_weight.shape[1] // out_weight.shape[0]
    features = keys.shape[1]
    quarter = resid.shape[1]
    model_width = down_weight.shape[1]

    hidden_width = gate_weight.shape[0]
    unit_rows_local = jnp.concatenate(
        [gate_weight.T, up_weight.T, down_weight, adapter_up.T], axis=1
    )
    unit_rows = lax.all_gather(unit_rows_local, "req", axis=0, tiled=True)
    gate_rows = unit_rows[:, :hidden_width]
    up_rows = unit_rows[:, hidden_width : 2 * hidden_width]
    down_rows = unit_rows[:, 2 * hidden_width : 2 * hidden_width + model_width]
    adapter_rows = unit_rows[:, 2 * hidden_width + model_width :]

    slot_count = keys.shape[0]
    block_count = block_table.shape[1]
    block_slots = slot_count // block_count
    table_row = block_table[0]
    placement = (jnp.arange(block_count)[:, None] == table_row[None, :]).astype(jnp.bfloat16)
    both = jnp.stack(
        [
            keys.reshape(block_count, block_slots, features),
            values.reshape(block_count, block_slots, features),
        ],
        axis=2,
    )
    ordered = jnp.einsum(
        "tj,jbkw->tbkw", placement, both, preferred_element_type=jnp.float32
    ).astype(jnp.bfloat16)
    per_dev = block_count // dec_count
    ordered = ordered.reshape(dec_count, per_dev, block_slots, 2, features)

    attn = attend(queries, keys, values, seg_ids)
    head_total = project_reduce_over_dec(attn, out_weight, dec_count)
    hidden = (resid.astype(jnp.float32) + head_total).astype(jnp.bfloat16)

    permuted = jnp.take(hidden, row_order[0], axis=0)
    cap = permuted.shape[0]
    req_n = unit_rows.shape[0] // gate_weight.shape[1]
    per_group = cap // req_n
    column = lax.all_to_all(
        permuted.reshape(req_n, per_group, quarter), "req", split_axis=0, concat_axis=0, tiled=True
    ).reshape(cap, quarter)
    spread = jnp.broadcast_to(column[None], (dec_count, cap, quarter))
    quarters = lax.all_to_all(spread, "dec", split_axis=0, concat_axis=0, tiled=True)
    mixed_rows = quarters.transpose(1, 0, 2).reshape(cap, dec_count * quarter)
    mixed_rows, ordered = lax.optimization_barrier((mixed_rows, ordered))
    moved = lax.all_to_all(ordered, "dec", split_axis=0, concat_axis=0, tiled=True)
    kv_cache = moved.transpose(1, 2, 3, 0, 4).reshape(per_dev, block_slots, 2 * dec_count * features)

    contract = (((1,), (1,)), ((), ()))
    halves = 2
    half = cap // halves
    outs = []
    for h in range(halves):
        values_f = mixed_rows[h * half : (h + 1) * half].astype(jnp.float32)
        scale = lax.rsqrt(jnp.mean(values_f * values_f, axis=-1, keepdims=True) + 1e-05)
        normed = (values_f * scale * norm_gain).astype(jnp.bfloat16)
        low_rank = jnp.dot(normed, adapter_down, preferred_element_type=jnp.float32).astype(
            jnp.bfloat16
        )
        gate = lax.dot_general(
            normed, gate_rows, contract, preferred_element_type=jnp.float32
        ) + lax.dot_general(low_rank, adapter_rows, contract, preferred_element_type=jnp.float32)
        up = lax.dot_general(normed, up_rows, contract, preferred_element_type=jnp.float32)
        hidden_units = (jax.nn.gelu(gate) * up).astype(jnp.bfloat16)
        down_part = jnp.dot(hidden_units, down_rows, preferred_element_type=jnp.float32).astype(
            jnp.bfloat16
        )
        mlp_total = reduce_over_dec(down_part, dec_count)
        own = column[h * half : (h + 1) * half].astype(jnp.float32)
        outs.append((own + mlp_total).astype(jnp.bfloat16))
    block_out = jnp.concatenate(outs, axis=0)
    return (block_out, kv_cache)


def solution(mesh):
    placed = (
        P("req", "dec"),
        P("req", "dec"),
        P("req", "dec"),
        P("req", "dec"),
        P("req"),
        P("dec", None),
        P(),
        P(),
        P(None, ("req", "dec")),
        P(None, ("req", "dec")),
        P(None, ("req", "dec")),
        P(("req", "dec"), None),
        P("req", None),
        P("req", None),
    )
    return jax.shard_map(
        body,
        mesh=mesh,
        in_specs=placed,
        out_specs=(P("req", "dec"), P(("req", "dec"), None, None)),
        check_vma=False,
    )
```

```python
import jax
import jax.numpy as jnp
from jax import lax
from jax.sharding import PartitionSpec as P

HD = 128


def attend(query_rows, key_rows, value_rows, segment):
    row_count = query_rows.shape[0]
    head_count = query_rows.shape[1] // HD
    query_heads = query_rows.reshape(row_count, head_count, HD)
    key_heads = key_rows.reshape(row_count, head_count, HD)
    value_heads = value_rows.reshape(row_count, head_count, HD)
    scores = jnp.einsum(
        "qhd,khd->hqk", query_heads, key_heads, preferred_element_type=jnp.float32
    ) * HD ** (-0.5)
    position = jnp.arange(row_count)
    allowed = (
        (segment[:, None] == segment[None, :])
        & (position[None, :] <= position[:, None])
        & (segment[:, None] >= 0)
    )
    masked = jnp.where(allowed[None], scores, -1e30)
    highest = jnp.max(masked, axis=-1, keepdims=True)
    exponent = jnp.where(allowed[None], jnp.exp(masked - highest), 0.0)
    denominator = jnp.sum(exponent, axis=-1, keepdims=True)
    denominator = jnp.where(denominator > 0, denominator, 1.0)
    weights = (exponent / denominator).astype(jnp.bfloat16)
    result = jnp.einsum("hqk,khd->qhd", weights, value_heads, preferred_element_type=jnp.float32)
    return result.astype(jnp.bfloat16).reshape(row_count, head_count * HD)


def project_reduce_over_dec(lhs, rhs, dec_count):
    quarter = rhs.shape[1] // dec_count
    here = lax.axis_index("dec")

    def quarter_of(index):
        block = lax.dynamic_slice_in_dim(rhs, index * quarter, quarter, 1)
        return jnp.dot(lhs, block, preferred_element_type=jnp.float32).astype(jnp.bfloat16)

    arrived = []
    for shift in range(1, dec_count):
        piece = quarter_of((here + shift) % dec_count)
        pairs = [(i, (i + shift) % dec_count) for i in range(dec_count)]
        arrived.append(lax.ppermute(piece, "dec", pairs))
    total = quarter_of(here).astype(jnp.float32)
    for piece in arrived:
        total = total + piece.astype(jnp.float32)
    return total


def reduce_over_dec(part, dec_count):
    quarter = part.shape[1] // dec_count
    here = lax.axis_index("dec")
    total = lax.dynamic_slice_in_dim(part, here * quarter, quarter, 1).astype(jnp.float32)
    for shift in range(1, dec_count):
        piece = lax.dynamic_slice_in_dim(part, ((here + shift) % dec_count) * quarter, quarter, 1)
        pairs = [(i, (i + shift) % dec_count) for i in range(dec_count)]
        total = total + lax.ppermute(piece, "dec", pairs).astype(jnp.float32)
    return total


def body(
    queries,
    keys,
    values,
    resid,
    seg_ids,
    out_weight,
    norm_gain,
    adapter_down,
    adapter_up,
    gate_weight,
    up_weight,
    down_weight,
    row_order,
    block_table,
):
    dec_count = out_weight.shape[1] // out_weight.shape[0]
    features = keys.shape[1]
    quarter = resid.shape[1]
    model_width = down_weight.shape[1]

    hidden_width = gate_weight.shape[0]
    unit_rows_local = jnp.concatenate(
        [gate_weight.T, up_weight.T, down_weight, adapter_up.T], axis=1
    )
    unit_rows = lax.all_gather(unit_rows_local, "req", axis=0, tiled=True)
    gate_rows = unit_rows[:, :hidden_width]
    up_rows = unit_rows[:, hidden_width : 2 * hidden_width]
    down_rows = unit_rows[:, 2 * hidden_width : 2 * hidden_width + model_width]
    adapter_rows = unit_rows[:, 2 * hidden_width + model_width :]

    slot_count = keys.shape[0]
    block_count = block_table.shape[1]
    block_slots = slot_count // block_count
    table_row = block_table[0]
    placement = (jnp.arange(block_count)[:, None] == table_row[None, :]).astype(jnp.bfloat16)
    both = jnp.stack(
        [
            keys.reshape(block_count, block_slots, features),
            values.reshape(block_count, block_slots, features),
        ],
        axis=2,
    )
    ordered = jnp.einsum(
        "tj,jbkw->tbkw", placement, both, preferred_element_type=jnp.float32
    ).astype(jnp.bfloat16)
    per_dev = block_count // dec_count
    ordered = ordered.reshape(dec_count, per_dev, block_slots, 2, features)

    attn = attend(queries, keys, values, seg_ids)
    head_total = project_reduce_over_dec(attn, out_weight, dec_count)
    hidden = (resid.astype(jnp.float32) + head_total).astype(jnp.bfloat16)

    permuted = jnp.take(hidden, row_order[0], axis=0)
    cap = permuted.shape[0]
    req_n = unit_rows.shape[0] // gate_weight.shape[1]
    per_group = cap // req_n
    column = lax.all_to_all(
        permuted.reshape(req_n, per_group, quarter), "req", split_axis=0, concat_axis=0, tiled=True
    ).reshape(cap, quarter)
    halves = 2
    half = cap // halves
    mixed_halves = []
    for h in range(halves):
        rows_h = column[h * half : (h + 1) * half]
        spread = jnp.broadcast_to(rows_h[None], (dec_count, half, quarter))
        quarters = lax.all_to_all(spread, "dec", split_axis=0, concat_axis=0, tiled=True)
        mixed_halves.append(quarters.transpose(1, 0, 2).reshape(half, dec_count * quarter))
    mixed_halves[-1], ordered = lax.optimization_barrier((mixed_halves[-1], ordered))
    moved = lax.all_to_all(ordered, "dec", split_axis=0, concat_axis=0, tiled=True)
    kv_cache = moved.transpose(1, 2, 3, 0, 4).reshape(per_dev, block_slots, 2 * dec_count * features)

    outs = []
    for h in range(halves):
        outs.append(mlp_half(h, mixed_halves[h], column, half, norm_gain, adapter_down, gate_rows,
                             adapter_rows, up_rows, down_rows, dec_count))
    block_out = jnp.concatenate(outs, axis=0)
    return (block_out, kv_cache)


def mlp_half(h, mixed, column, half, norm_gain, adapter_down, gate_rows, adapter_rows, up_rows,
             down_rows, dec_count):
    contract = (((1,), (1,)), ((), ()))
    values_f = mixed.astype(jnp.float32)
    scale = lax.rsqrt(jnp.mean(values_f * values_f, axis=-1, keepdims=True) + 1e-05)
    normed = (values_f * scale * norm_gain).astype(jnp.bfloat16)
    low_rank = jnp.dot(normed, adapter_down, preferred_element_type=jnp.float32).astype(
        jnp.bfloat16
    )
    gate = lax.dot_general(
        normed, gate_rows, contract, preferred_element_type=jnp.float32
    ) + lax.dot_general(low_rank, adapter_rows, contract, preferred_element_type=jnp.float32)
    up = lax.dot_general(normed, up_rows, contract, preferred_element_type=jnp.float32)
    hidden_units = (jax.nn.gelu(gate) * up).astype(jnp.bfloat16)
    down_part = jnp.dot(hidden_units, down_rows, preferred_element_type=jnp.float32).astype(
        jnp.bfloat16
    )
    mlp_total = reduce_over_dec(down_part, dec_count)
    own = column[h * half : (h + 1) * half].astype(jnp.float32)
    return (own + mlp_total).astype(jnp.bfloat16)


def solution(mesh):
    placed = (
        P("req", "dec"),
        P("req", "dec"),
        P("req", "dec"),
        P("req", "dec"),
        P("req"),
        P("dec", None),
        P(),
        P(),
        P(None, ("req", "dec")),
        P(None, ("req", "dec")),
        P(None, ("req", "dec")),
        P(("req", "dec"), None),
        P("req", None),
        P("req", None),
    )
    return jax.shard_map(
        body,
        mesh=mesh,
        in_specs=placed,
        out_specs=(P("req", "dec"), P(("req", "dec"), None, None)),
        check_vma=False,
    )
```
